32 devices in a mesh: groups: 2 (over y), seq: 4 (over z), chan: 2 (over x), rep: 2 (over core).
Axes of the slice: x: 2, y: 2, z: 4, core: 2. Of those that a mesh axis runs over, the one named last changes fastest.
Arguments:
- projected: bfloat16 [4096, 3, 8192], P(('groups', 'seq'), None, ('chan', 'rep')), parts along dimension 0, may hold values from -6 to 6
- short_weight: float32 [3, 3, 8192], P(None, None, ('chan', 'rep')), may hold values from -3.5 to 3.5
- skip_gain: float32 [8192], P(('chan', 'rep')), may hold values from -4 to 4
- pole_rate: float32 [16, 512], P(None, ('chan', 'rep')), may hold values from 2.4414062e-06 to 0.03
- residue: float32 [16, 512], P(None, ('chan', 'rep')), may hold values from -0.088388346 to 0.088388346
- out_weight: bfloat16 [2, 2, 2048, 4096], P(None, 'rep', 'seq', 'chan'), may hold values from -0.0625 to 0.0625
Outputs:
- mixed: bfloat16 [4096, 4096], P(('groups', 'seq'), ('chan', 'rep')), parts along dimension 0
The draws below stay inside these ranges and needn't reach their ends.
There are 2 independent parts, one for each index of `groups`. The reference program is written for one: setup_inputs(seed, part) draws one part's arguments, and reference() takes and returns one part's arrays. A program takes and returns all parts, laid end to end along the dimension named above; an argument that names none is the same for every part. Nothing has to cross between parts.
All inputs are finite; a program needn't handle non-finite values.
Results may differ from the reference program's by a relative error of at most 0.005.
Values may be sent and summed in bfloat16 or wider, within the bound.
A program may use at most 128 MiB of HBM per device.

```python
import math
import jax
import jax.numpy as jnp
from jax import lax

D = 8192
ORDER = 16
DOUT = 4096
BLOCK = 128
SEQ_LEN = 2048
GROUPS = 512
N_CHAN = 2
N_REP = 2


def level_of(own_key, shape, shards, low, top_value):
    def one(dim, blocks):
        draws = jax.random.uniform(jax.random.fold_in(jax.random.fold_in(own_key, 6), dim), (blocks,), jnp.float32, low / len(shards), top_value / len(shards))
        return jnp.repeat(jnp.exp(draws), shape[dim] // blocks).reshape((-1,) + (1,) * (len(shape) - dim - 1))

    level = one(*shards[0])
    for cut in shards[1:]:
        level = level * one(*cut)
    return level


def bell_draw(own_key, shape, deviation, limit, cuts=(), kind=jnp.bfloat16):
    array = jax.random.normal(own_key, shape, jnp.float32) * deviation
    if len(cuts) > 0:
        array = level_of(own_key, shape, cuts, -0.22, 0.18) * array
    return jnp.clip(array, min=-limit, max=limit).astype(kind)


def setup_inputs(seed: int = 0, part: int = 0) -> dict:
    arg_keys = jax.random.split(jax.random.key(seed), 7)
    part_splits = jax.random.split(jax.random.fold_in(arg_keys[6], part), 7)
    return {
        "projected": bell_draw(part_splits[0], (SEQ_LEN, 3, D), 1.0, 6.0, ((0, 4), (2, 4))),
        "short_weight": bell_draw(arg_keys[1], (3, 3, D), 3 ** -0.5, 3.5, ((2, 4),), jnp.float32),
        "skip_gain": bell_draw(arg_keys[2], (D,), 1.0, 4.0, ((0, 4),), jnp.float32),
        "pole_rate": jnp.clip(jnp.exp(math.log(0.03) - 9.416378 * jax.random.uniform(arg_keys[3], (ORDER, GROUPS), jnp.float32) ** level_of(arg_keys[3], (ORDER, GROUPS), ((1, 4),), -0.2, 0.2)), 2.441406195430318e-06, 0.03),
        "residue": bell_draw(arg_keys[4], (ORDER, GROUPS), (0.3 * SEQ_LEN ** -0.5), 0.088388346, ((1, 4),), jnp.float32),
        "out_weight": bell_draw(arg_keys[5], (N_CHAN, N_REP, D // (N_CHAN * N_REP), DOUT), D ** -0.5, 0.0625, ((1, 2), (2, 4), (3, 2))),
    }


def filter_tables(decay_rate, residue, block_len):
    offsets = jnp.arange(block_len, dtype=jnp.int32)
    lag_diff = offsets[:, None] - offsets[None, :]
    lag_float = jnp.maximum(lag_diff, 0).astype(decay_rate.dtype)
    kernel = jnp.zeros((decay_rate.shape[1], block_len, block_len), decay_rate.dtype)
    for order_idx in range(decay_rate.shape[0]):
        kernel = kernel + residue[order_idx][:, None, None] * jnp.exp(-decay_rate[order_idx][:, None, None] * lag_float[None])
    kernel = jnp.where(lag_diff[None] >= 0, kernel, jnp.zeros_like(kernel))
    rate_t = decay_rate.T
    ahead = (offsets + 1).astype(decay_rate.dtype)
    readout = residue.T[:, None, :] * jnp.exp(-rate_t[:, None, :] * ahead[None, :, None])
    behind = (block_len - 1 - offsets).astype(decay_rate.dtype)
    intake = jnp.exp(-rate_t[:, :, None] * behind[None, None, :])
    return kernel, readout, intake


def block_conv(product, decay_rate, residue):
    groups = decay_rate.shape[1]
    group_size = product.shape[1] // groups
    kernel, readout, intake = filter_tables(decay_rate, residue, BLOCK)
    step_decay = jnp.exp(-decay_rate * BLOCK)[:, :, None]
    num_blocks = product.shape[0] // BLOCK
    blocks_in = product.reshape(num_blocks, BLOCK, groups, group_size)
    highest = lax.Precision.HIGHEST

    def block_step(carry_state, block_in):
        inside = jnp.einsum('gij,jgc->igc', kernel, block_in, precision=highest)
        across = jnp.einsum('gin,ngc->igc', readout, carry_state, precision=highest)
        updated = step_decay * carry_state + jnp.einsum('gnj,jgc->ngc', intake, block_in, precision=highest)
        return updated, inside + across

    start_state = jnp.zeros((decay_rate.shape[0], groups, group_size), jnp.float32)
    final_state, outputs = lax.scan(block_step, start_state, blocks_in)
    return outputs.reshape(product.shape)


def reference(projected, short_weight, skip_gain, pole_rate, residue, out_weight):
    features = projected.astype(jnp.float32)
    padded = jnp.pad(features, ((2, 0), (0, 0), (0, 0)))
    length = features.shape[0]
    filtered = short_weight[:, 0][None] * features + short_weight[:, 1][None] * padded[1:length + 1] + short_weight[:, 2][None] * padded[:length]
    query_part = filtered[:, 0]
    key_part = filtered[:, 1]
    value_part = filtered[:, 2]
    product = key_part * value_part
    conv = block_conv(product, pole_rate, residue)
    gated_out = (query_part * (conv + skip_gain[None] * product)).astype(jnp.bfloat16)
    full_weight = out_weight.reshape(-1, out_weight.shape[3])
    return jnp.dot(gated_out, full_weight, preferred_element_type=jnp.float32).astype(jnp.bfloat16)
```

```python
import functools

import jax
import jax.numpy as jnp
from jax import lax
from jax.experimental import pallas as pl
from jax.experimental.pallas import tpu as pltpu
from jax.sharding import PartitionSpec as P

GROUP = 16
LANES = 128
BLOCK = 128
PER_TILE = LANES // GROUP


def masked_rows(rows):
    lane_group = lax.broadcasted_iota(jnp.int32, rows.shape, 1) // GROUP
    zero = jnp.zeros_like(rows)
    return jnp.concatenate(
        [jnp.where(lane_group == g, rows, zero) for g in range(PER_TILE)], axis=0
    )


def readout_table(rate_row, res_row):
    ahead = (lax.broadcasted_iota(jnp.int32, (BLOCK, rate_row.shape[1]), 0) + 1).astype(jnp.float32)
    return res_row * jnp.exp(-rate_row * ahead)


def conv_body(x_ref, halo_ref, sw_ref, skip_ref, rate_rep_ref, res_rep_ref, rate_row_ref,
              res_row_ref, rate_ch_ref, q_ref, base_ref, end_ref, ext, lhs):
    tok = x_ref.shape[1]
    blocks = tok // BLOCK
    modes = rate_ch_ref.shape[0]

    def short(s):
        x = x_ref[s].astype(jnp.float32)
        ext[8:, :] = x
        ext[6:8, :] = halo_ref[s].astype(jnp.float32)
        return (
            sw_ref[s, 0:1, :] * x
            + sw_ref[s, 1:2, :] * ext[7 : tok + 7, :]
            + sw_ref[s, 2:3, :] * ext[6 : tok + 6, :]
        )

    q_ref[...] = short(0)
    product = short(1)
    product = product * short(2)

    lane = lax.broadcasted_iota(jnp.int32, rate_rep_ref.shape, 1) % BLOCK
    rate_rep = rate_rep_ref[...]
    back = ((BLOCK - lane) % BLOCK).astype(jnp.float32)
    row = jnp.sum(res_rep_ref[...] * jnp.exp(-rate_rep * back), axis=0, keepdims=True)
    lower = lax.broadcasted_iota(jnp.int32, (BLOCK, BLOCK), 1) <= lax.broadcasted_iota(
        jnp.int32, (BLOCK, BLOCK), 0
    )
    for g in range(PER_TILE):
        cols = slice(g * BLOCK, (g + 1) * BLOCK)
        wide = jnp.broadcast_to(row[:, cols], (BLOCK, BLOCK))
        table = pltpu.roll(wide, 0, 1, stride=1, stride_axis=0)
        lhs[:BLOCK, cols] = jnp.where(lower, table, 0.0).astype(jnp.bfloat16)
    lhs[BLOCK:, :] = jnp.exp(-rate_rep * (BLOCK - 1 - lane).astype(jnp.float32)).astype(jnp.bfloat16)

    decay = jnp.exp(-rate_ch_ref[...] * BLOCK)
    readout = readout_table(rate_row_ref[...], res_row_ref[...]).astype(jnp.bfloat16)
    state = jnp.zeros((modes, LANES), jnp.float32)
    for b in range(blocks):
        rows = slice(b * BLOCK, (b + 1) * BLOCK)
        p_b = product[rows]
        out = jnp.dot(lhs[...], masked_rows(p_b.astype(jnp.bfloat16)), preferred_element_type=jnp.float32)
        value = out[:BLOCK] + skip_ref[...] * p_b
        if b > 0:
            value = value + jnp.dot(
                readout, masked_rows(state.astype(jnp.bfloat16)), preferred_element_type=jnp.float32
            )
        base_ref[rows, :] = value
        state = decay * state + out[BLOCK:]
    end_ref[...] = state


def gate_body(q_ref, base_ref, prior_ref, rate_row_ref, res_row_ref, rate_ch_ref, out_ref):
    readout = readout_table(rate_row_ref[...], res_row_ref[...]).astype(jnp.bfloat16)
    decay = jnp.exp(-rate_ch_ref[...] * BLOCK)
    state = prior_ref[...]
    for b in range(q_ref.shape[0] // BLOCK):
        rows = slice(b * BLOCK, (b + 1) * BLOCK)
        across = jnp.dot(
            readout, masked_rows(state.astype(jnp.bfloat16)), preferred_element_type=jnp.float32
        )
        out_ref[rows, :] = (q_ref[rows, :] * (base_ref[rows, :] + across)).astype(jnp.bfloat16)
        state = decay * state


def project_body(a_ref, w_ref, out_ref):
    @pl.when((pl.program_id(1) == 0) & (pl.program_id(2) == 0))
    def _():
        out_ref[...] = jnp.zeros_like(out_ref)

    w = w_ref[...].reshape(-1, w_ref.shape[-1])
    out_ref[...] += jnp.dot(a_ref[0], w, preferred_element_type=jnp.float32)


def per_device(projected, short_weight, skip_gain, pole_rate, residue, out_weight):
    tok = projected.shape[0]
    chans = projected.shape[2]
    modes, groups = pole_rate.shape
    tiles = chans // LANES
    count = lax.axis_size("seq")
    slabs = lax.axis_size("groups")
    n_chan = out_weight.shape[0]
    local_rows = out_weight.shape[2]
    out_cols = out_weight.shape[3]
    half = out_cols // slabs
    wide = PER_TILE * BLOCK

    mine = lax.dynamic_slice_in_dim(
        out_weight[:, 0], lax.axis_index("groups") * half, half, axis=2
    )
    weight = lax.all_gather(mine, ("groups", "seq"), axis=0)
    weight = weight.reshape(slabs, count, n_chan, local_rows, half)

    x = projected.transpose(1, 0, 2)
    halo = lax.ppermute(x[:, tok - 2 :], "seq", [(i, i + 1) for i in range(count - 1)])
    rate_rep = jnp.repeat(pole_rate, BLOCK, axis=1)
    res_rep = jnp.repeat(residue, BLOCK, axis=1)
    rate_row = pole_rate.T.reshape(1, -1)
    res_row = residue.T.reshape(1, -1)
    rate_ch = jnp.repeat(pole_rate, GROUP, axis=1)

    def spec(*lead, width=LANES):
        return pl.BlockSpec((*lead, width), lambda t: (0,) * len(lead) + (t,))

    q, base, end = pl.pallas_call(
        conv_body,
        grid=(tiles,),
        in_specs=[
            spec(3, tok), spec(3, 2), spec(3, 3), spec(1), spec(modes, width=wide),
            spec(modes, width=wide), spec(1), spec(1), spec(modes),
        ],
        out_specs=[spec(tok), spec(tok), spec(modes)],
        out_shape=[
            jax.ShapeDtypeStruct((tok, chans), jnp.float32),
            jax.ShapeDtypeStruct((tok, chans), jnp.float32),
            jax.ShapeDtypeStruct((modes, chans), jnp.float32),
        ],
        scratch_shapes=[
            pltpu.VMEM((tok + 8, LANES), jnp.float32),
            pltpu.VMEM((BLOCK + modes, wide), jnp.bfloat16),
        ],
        cost_estimate=pl.CostEstimate(
            flops=2 * tok * chans * 1152, bytes_accessed=14 * tok * chans, transcendentals=0
        ),
        name="conv_local",
    )(x, halo, short_weight, skip_gain[None], rate_rep, res_rep, rate_row, res_row, rate_ch)

    ends = lax.all_gather(end, "seq", axis=0)
    distance = lax.axis_index("seq") - 1 - jnp.arange(count, dtype=jnp.int32)
    spans = (tok * jnp.maximum(distance, 0)).astype(jnp.float32)
    factors = jnp.exp(-rate_ch[None] * spans[:, None, None])
    prior = jnp.sum(jnp.where((distance >= 0)[:, None, None], factors * ends, 0.0), axis=0)

    gated = pl.pallas_call(
        gate_body,
        grid=(tiles,),
        in_specs=[spec(tok), spec(tok), spec(modes), spec(1), spec(1), spec(modes)],
        out_specs=spec(tok),
        out_shape=jax.ShapeDtypeStruct((tok, chans), jnp.bfloat16),
        cost_estimate=pl.CostEstimate(
            flops=2 * tok * chans * 128, bytes_accessed=10 * tok * chans, transcendentals=0
        ),
        name="gate",
    )(q, base, prior, rate_row, res_row, rate_ch)

    full = lax.all_gather(gated, "chan", axis=0)
    step = max(1, LANES // local_rows)
    depth = step * local_rows
    partial_sum = pl.pallas_call(
        project_body,
        grid=(slabs, n_chan, count // step),
        in_specs=[
            pl.BlockSpec((1, tok, depth), lambda g, c, s: (c, 0, s)),
            pl.BlockSpec((1, step, 1, local_rows, half), lambda g, c, s: (g, s, c, 0, 0)),
        ],
        out_specs=pl.BlockSpec((tok, half), lambda g, c, s: (0, g)),
        out_shape=jax.ShapeDtypeStruct((tok, out_cols), jnp.float32),
        cost_estimate=pl.CostEstimate(
            flops=2 * tok * n_chan * chans * out_cols,
            bytes_accessed=2 * n_chan * chans * out_cols + 4 * tok * out_cols,
            transcendentals=0,
        ),
        name="project",
    )(full, weight)
    return lax.psum_scatter(partial_sum, "rep", scatter_dimension=1, tiled=True).astype(
        jnp.bfloat16
    )


def solution(mesh):
    return jax.shard_map(
        per_device,
        mesh=mesh,
        in_specs=(
            P(("groups", "seq"), None, ("chan", "rep")),
            P(None, None, ("chan", "rep")),
            P(("chan", "rep")),
            P(None, ("chan", "rep")),
            P(None, ("chan", "rep")),
            P(None, "rep", "seq", "chan"),
        ),
        out_specs=P(("groups", "seq"), ("chan", "rep")),
        check_vma=False,
    )
```

```python
import functools

import jax
import jax.numpy as jnp
from jax import lax
from jax.experimental import pallas as pl
from jax.experimental.pallas import tpu as pltpu
from jax.sharding import PartitionSpec as P

GROUP = 16
LANES = 128
BLOCK = 128
PER_TILE = LANES // GROUP
WIDE = PER_TILE * BLOCK
HALO = 16
MESH = pl.DeviceIdType.MESH
HIGHEST = lax.Precision.HIGHEST


def iota(shape, dim):
    return lax.broadcasted_iota(jnp.int32, shape, dim)


def masked_rows(rows):
    lane_group = iota(rows.shape, 1) // GROUP
    zero = jnp.zeros_like(rows)
    return jnp.concatenate(
        [jnp.where(lane_group == g, rows, zero) for g in range(PER_TILE)], axis=0
    )


def kernel(dims, x_hbm, sw_ref, skip_ref, rate_ref, res_ref, w_hbm, out_ref,
           xbuf, halo, ext, lhs, q_buf, base, ends, own_end, prior, rate_ch, readout, gated, wbuf,
           acc, peer, local_sem, halo_sem, end_send, end_recv, gate_send, gate_recv,
           zsend, zrecv, ysend, yrecv, rep_send, rep_recv):
    count, slabs, n_chan, n_rep, chunks, row_chunks = dims
    tok, chans = gated.shape[1], gated.shape[2]
    modes, groups = rate_ref.shape
    tiles = chans // LANES
    blocks = tok // BLOCK
    local_rows, out_cols = w_hbm.shape[2], w_hbm.shape[3]
    half = out_cols // slabs
    rows = local_rows // row_chunks
    out_half = out_cols // n_rep
    slab = lax.axis_index("groups")
    seq = lax.axis_index("seq")
    chan = lax.axis_index("chan")
    rep = lax.axis_index("rep")
    other_slab = 1 - slab
    other_rep = 1 - rep

    barrier = pltpu.get_barrier_semaphore()

    def greet(target):
        pl.semaphore_signal(barrier, inc=1, device_id=target, device_id_type=MESH)

    for d in range(1, count):
        greet({"seq": lax.rem(seq + d, count)})
    for d in range(1, n_chan):
        greet({"chan": lax.rem(chan + d, n_chan)})
    greet({"groups": other_slab})
    greet({"rep": other_rep})
    pl.semaphore_wait(barrier, count + n_chan)

    def piece(ref, c, r, h):
        cols = pl.ds(pl.multiple_of(h * half, LANES), half)
        if chunks == 1:
            return ref.at[:, :, cols]
        return ref.at[c, pl.ds(pl.multiple_of(r * rows, rows), rows), cols]

    def split(ch):
        return ch // row_chunks, ch % row_chunks

    def own_piece(ch):
        c, r = split(ch)
        return piece(w_hbm.at[:, 0], c, r, slab)

    def block_piece(b, ch, h):
        c, r = split(ch)
        return piece(wbuf.at[b], c, r, h)

    def target_of(direction):
        return seq + 1 if direction == 0 else seq - 1

    def can_send(direction):
        return seq < count - 1 if direction == 0 else seq > 0

    def origin(direction, k):
        return seq - 1 - k if direction == 0 else seq + 1 + k

    def has(direction, k):
        return seq - 1 - k >= 0 if direction == 0 else seq + 1 + k < count

    def z_copy(direction, k, ch, src, b):
        return pltpu.make_async_remote_copy(
            src_ref=src, dst_ref=block_piece(b, ch, slab),
            send_sem=zsend.at[direction, k, ch], recv_sem=zrecv.at[direction, k, ch],
            device_id={"seq": target_of(direction)}, device_id_type=MESH,
        )

    def y_copy(direction, k, ch, h):
        b = origin(direction, k)
        ref = block_piece(b, ch, h)
        return pltpu.make_async_remote_copy(
            src_ref=ref, dst_ref=ref,
            send_sem=ysend.at[direction, k, ch], recv_sem=yrecv.at[direction, k, ch],
            device_id={"groups": other_slab}, device_id_type=MESH,
        )

    def halo_copy():
        return pltpu.make_async_remote_copy(
            src_ref=x_hbm.at[:, pl.ds(tok - HALO, HALO), :], dst_ref=halo,
            send_sem=halo_sem.at[0], recv_sem=halo_sem.at[1],
            device_id={"seq": seq + 1}, device_id_type=MESH,
        )

    @pl.when(seq < count - 1)
    def _():
        halo_copy().start()

    for ch in range(chunks):
        for direction in (0, 1):
            @pl.when(can_send(direction))
            def _():
                z_copy(direction, 0, ch, own_piece(ch), seq).start()

    x_copy = pltpu.make_async_copy(x_hbm, xbuf, local_sem.at[0])
    x_copy.start()
    w_copy = pltpu.make_async_copy(w_hbm.at[:, 0], wbuf.at[seq], local_sem.at[1])
    w_copy.start()
    x_copy.wait()

    @pl.when(seq > 0)
    def _():
        halo_copy().wait_recv()

    @pl.when(seq == 0)
    def _():
        halo[...] = jnp.zeros_like(halo)

    def pump(k, ch):
        for direction in (0, 1):
            @pl.when(has(direction, k))
            def _():
                b = origin(direction, k)
                landed = block_piece(b, ch, slab)
                z_copy(direction, k, ch, landed, b).wait_recv()
                y_copy(direction, k, ch, slab).start()

                @pl.when(can_send(direction))
                def _():
                    z_copy(direction, k + 1, ch, landed, b).start()

    def conv_tile(t, carry):
        cols = pl.ds(pl.multiple_of(t * LANES, LANES), LANES)

        def short(s):
            x = xbuf[s, :, cols].astype(jnp.float32)
            ext[HALO:, :] = x
            ext[:HALO, :] = halo[s, :, cols].astype(jnp.float32)
            return (
                sw_ref[s, 0:1, cols] * x
                + sw_ref[s, 1:2, cols] * ext[HALO - 1 : tok + HALO - 1, :]
                + sw_ref[s, 2:3, cols] * ext[HALO - 2 : tok + HALO - 2, :]
            )

        q_buf[:, cols] = short(0)
        product = short(1)
        product = product * short(2)

        pick_wide = (
            iota((groups, WIDE), 0) == t * PER_TILE + iota((groups, WIDE), 1) // BLOCK
        ).astype(jnp.float32)
        pick = (
            iota((groups, LANES), 0) == t * PER_TILE + iota((groups, LANES), 1) // GROUP
        ).astype(jnp.float32)

        def spread(table, which):
            return jnp.dot(table, which, precision=HIGHEST, preferred_element_type=jnp.float32)

        rate, res = rate_ref[...], res_ref[...]
        rate_rep, res_rep = spread(rate, pick_wide), spread(res, pick_wide)
        rate_c, res_c = spread(rate, pick), spread(res, pick)
        diagonal = iota((modes, LANES), 0) == iota((modes, LANES), 1) % GROUP
        rate_row = jnp.sum(jnp.where(diagonal, rate_c, 0.0), axis=0, keepdims=True)
        res_row = jnp.sum(jnp.where(diagonal, res_c, 0.0), axis=0, keepdims=True)
        ahead = (iota((BLOCK, LANES), 0) + 1).astype(jnp.float32)
        read = (res_row * jnp.exp(-rate_row * ahead)).astype(jnp.bfloat16)

        lane = iota((modes, WIDE), 1) % BLOCK
        back = ((BLOCK - lane) % BLOCK).astype(jnp.float32)
        row = jnp.sum(res_rep * jnp.exp(-rate_rep * back), axis=0, keepdims=True)
        lower = iota((BLOCK, BLOCK), 1) <= iota((BLOCK, BLOCK), 0)
        for g in range(PER_TILE):
            part = slice(g * BLOCK, (g + 1) * BLOCK)
            wide = jnp.broadcast_to(row[:, part], (BLOCK, BLOCK))
            table = pltpu.roll(wide, 0, 1, stride=1, stride_axis=0)
            lhs[:BLOCK, part] = jnp.where(lower, table, 0.0).astype(jnp.bfloat16)
        lhs[BLOCK:, :] = jnp.exp(-rate_rep * (BLOCK - 1 - lane).astype(jnp.float32)).astype(
            jnp.bfloat16
        )

        decay = jnp.exp(-rate_c * BLOCK)
        state = jnp.zeros((modes, LANES), jnp.float32)
        for b in range(blocks):
            rows_b = slice(b * BLOCK, (b + 1) * BLOCK)
            p_b = product[rows_b]
            made = jnp.dot(
                lhs[...], masked_rows(p_b.astype(jnp.bfloat16)), preferred_element_type=jnp.float32
            )
            value = made[:BLOCK] + skip_ref[:, cols] * p_b
            if b > 0:
                value = value + jnp.dot(
                    read, masked_rows(state.astype(jnp.bfloat16)), preferred_element_type=jnp.float32
                )
            base[rows_b, cols] = value
            state = decay * state + made[BLOCK:]
        own_end[:, cols] = state
        rate_ch[:, cols] = rate_c
        readout[:, cols] = read
        return carry

    steps = [(k, ch) for k in range(count - 1) for ch in range(chunks)]
    early = 3 if len(steps) > 3 and chunks >= 3 else 1
    part = tiles // (early + 1)
    for e in range(early + 1):
        stop = tiles if e == early else (e + 1) * part
        lax.fori_loop(e * part, stop, conv_tile, 0)
        if e < early:
            pump(*steps[e])

    def end_copy(d):
        return pltpu.make_async_remote_copy(
            src_ref=own_end, dst_ref=ends.at[seq],
            send_sem=end_send.at[d], recv_sem=end_recv.at[seq],
            device_id={"seq": seq + d}, device_id_type=MESH,
        )

    def arrived_end(source):
        return pltpu.make_async_remote_copy(
            src_ref=own_end, dst_ref=ends.at[source],
            send_sem=end_send.at[0], recv_sem=end_recv.at[source],
            device_id={"seq": seq - 1}, device_id_type=MESH,
        )

    for d in range(1, count):
        @pl.when(seq + d < count)
        def _():
            end_copy(d).start()

    prior[...] = jnp.zeros_like(prior)
    for source in range(count - 1):
        @pl.when(source < seq)
        def _():
            arrived_end(source).wait_recv()
            prior[...] = prior[...] * jnp.exp(-rate_ch[...] * tok) + ends[source]

    def gate_tile(t, carry):
        cols = pl.ds(pl.multiple_of(t * LANES, LANES), LANES)
        read = readout[:, cols]
        decay = jnp.exp(-rate_ch[:, cols] * BLOCK)
        state = prior[:, cols]
        for b in range(blocks):
            rows_b = slice(b * BLOCK, (b + 1) * BLOCK)
            across = jnp.dot(
                read, masked_rows(state.astype(jnp.bfloat16)), preferred_element_type=jnp.float32
            )
            gated[chan, rows_b, cols] = (
                q_buf[rows_b, cols] * (base[rows_b, cols] + across)
            ).astype(jnp.bfloat16)
            state = decay * state
        return carry

    lax.fori_loop(0, tiles, gate_tile, 0)

    def gate_copy(d):
        return pltpu.make_async_remote_copy(
            src_ref=gated.at[chan], dst_ref=gated.at[chan],
            send_sem=gate_send.at[d], recv_sem=gate_recv.at[chan],
            device_id={"chan": lax.rem(chan + d, n_chan)}, device_id_type=MESH,
        )

    def arrived_gate(d):
        source = lax.rem(chan + d, n_chan)
        return pltpu.make_async_remote_copy(
            src_ref=gated.at[source], dst_ref=gated.at[source],
            send_sem=gate_send.at[0], recv_sem=gate_recv.at[source],
            device_id={"chan": source}, device_id_type=MESH,
        )

    for d in range(1, n_chan):
        gate_copy(d).start()

    middle = min(len(steps), early + 3)
    for e in range(early, middle):
        pump(*steps[e])
    acc[...] = jnp.zeros_like(acc)
    w_copy.wait()
    for d in range(1, n_chan):
        arrived_gate(d).wait_recv()

    streamed = chunks > 1
    col_tile = min(512, out_cols)

    def multiply(b, ch):
        c, r = split(ch)
        a = gated[c, :, pl.ds(pl.multiple_of(b * local_rows + r * rows, LANES), rows)]

        def column(n, carry):
            cols = pl.ds(pl.multiple_of(n * col_tile, col_tile), col_tile)
            w = wbuf[b, c, pl.ds(pl.multiple_of(r * rows, rows), rows), cols]
            acc[:, cols] += jnp.dot(a, w, preferred_element_type=jnp.float32)
            return carry

        lax.fori_loop(0, out_cols // col_tile, column, 0)

    def consume(k, ch):
        for direction in (0, 1):
            @pl.when(has(direction, k))
            def _():
                y_copy(direction, k, ch, other_slab).wait_recv()
                if streamed:
                    multiply(origin(direction, k), ch)

    if streamed:
        lax.fori_loop(0, chunks, lambda ch, carry: (multiply(seq, ch), carry)[1], 0)

    def both(j, carry):
        pump(j // chunks, j % chunks)
        old = j - 1
        consume(old // chunks, old % chunks)
        return carry

    def only(j, carry):
        consume(j // chunks, j % chunks)
        return carry

    total = len(steps)
    lax.fori_loop(0, middle - 1, only, 0)
    lax.fori_loop(middle, total, both, 0)
    lax.fori_loop(total - 1, total, only, 0)

    if not streamed:
        def whole_column(n, carry):
            cols = pl.ds(pl.multiple_of(n * half, half), half)
            for c in range(n_chan):
                w = wbuf[:, c, :, cols].reshape(count * local_rows, half)
                acc[:, cols] += jnp.dot(gated[c], w, preferred_element_type=jnp.float32)
            return carry

        lax.fori_loop(0, slabs, whole_column, 0)

    quarter = tok // 4

    def rep_copy(i, side):
        return pltpu.make_async_remote_copy(
            src_ref=acc.at[
                pl.ds(i * quarter, quarter), pl.ds(pl.multiple_of(side * out_half, LANES), out_half)
            ],
            dst_ref=peer.at[pl.ds(i * quarter, quarter), :],
            send_sem=rep_send.at[i], recv_sem=rep_recv.at[i],
            device_id={"rep": other_rep}, device_id_type=MESH,
        )

    for i in range(4):
        rep_copy(i, other_rep).start()
    mine = pl.ds(pl.multiple_of(rep * out_half, LANES), out_half)
    for i in range(4):
        rep_copy(i, other_rep).wait_recv()
        rows_i = pl.ds(i * quarter, quarter)
        out_ref[rows_i, :] = (acc[rows_i, mine] + peer[rows_i, :]).astype(jnp.bfloat16)

    for i in range(4):
        rep_copy(i, other_rep).wait_send()
    for d in range(1, n_chan):
        gate_copy(d).wait_send()
    for d in range(1, count):
        @pl.when(seq + d < count)
        def _():
            end_copy(d).wait_send()

    @pl.when(seq < count - 1)
    def _():
        halo_copy().wait_send()

    for ch in range(chunks):
        for direction in (0, 1):
            @pl.when(can_send(direction))
            def _():
                z_copy(direction, 0, ch, own_piece(ch), seq).wait_send()

    def drain(j, carry):
        k, ch = j // chunks, j % chunks
        for direction in (0, 1):
            @pl.when(has(direction, k))
            def _():
                y_copy(direction, k, ch, slab).wait_send()

                @pl.when(can_send(direction))
                def _():
                    b = origin(direction, k)
                    z_copy(direction, k + 1, ch, block_piece(b, ch, slab), b).wait_send()
        return carry

    lax.fori_loop(0, total, drain, 0)


def per_device(projected, short_weight, skip_gain, pole_rate, residue, out_weight):
    tok, _, chans = projected.shape
    modes, groups = pole_rate.shape
    n_chan, _, local_rows, out_cols = out_weight.shape
    count, slabs = lax.axis_size("seq"), lax.axis_size("groups")
    n_rep = lax.axis_size("rep")
    row_chunks = max(1, local_rows // 256)
    chunks = n_chan * row_chunks if local_rows % LANES == 0 else 1
    dims = (count, slabs, n_chan, n_rep, chunks, row_chunks)
    f32, bf16 = jnp.float32, jnp.bfloat16
    dma = pltpu.SemaphoreType.DMA
    anywhere = pl.BlockSpec(memory_space=pl.ANY)
    vmem = pl.BlockSpec(memory_space=pltpu.VMEM)
    return pl.pallas_call(
        functools.partial(kernel, dims),
        in_specs=[anywhere, vmem, vmem, vmem, vmem, anywhere],
        out_specs=vmem,
        out_shape=jax.ShapeDtypeStruct((tok, out_cols // n_rep), bf16),
        scratch_shapes=[
            pltpu.VMEM((3, tok, chans), bf16),
            pltpu.VMEM((3, HALO, chans), bf16),
            pltpu.VMEM((tok + HALO, LANES), f32),
            pltpu.VMEM((BLOCK + modes, WIDE), bf16),
            pltpu.VMEM((tok, chans), f32),
            pltpu.VMEM((tok, chans), f32),
            pltpu.VMEM((count, modes, chans), f32),
            pltpu.VMEM((modes, chans), f32),
            pltpu.VMEM((modes, chans), f32),
            pltpu.VMEM((modes, chans), f32),
            pltpu.VMEM((BLOCK, chans), bf16),
            pltpu.VMEM((n_chan, tok, chans), bf16),
            pltpu.VMEM((count, n_chan, local_rows, out_cols), bf16),
            pltpu.VMEM((tok, out_cols), f32),
            pltpu.VMEM((tok, out_cols // n_rep), f32),
            dma((2,)),
            dma((2,)),
            dma((count,)),
            dma((count,)),
            dma((n_chan,)),
            dma((n_chan,)),
            dma((2, count, chunks)),
            dma((2, count, chunks)),
            dma((2, count, chunks)),
            dma((2, count, chunks)),
            dma((4,)),
            dma((4,)),
        ],
        compiler_params=pltpu.CompilerParams(
            collective_id=0, has_side_effects=True, vmem_limit_bytes=60 * 1024 * 1024
        ),
        name="hyena",
    )(
        projected.transpose(1, 0, 2), short_weight, skip_gain[None], pole_rate, residue, out_weight
    )


def solution(mesh):
    return jax.shard_map(
        per_device,
        mesh=mesh,
        in_specs=(
            P(("groups", "seq"), None, ("chan", "rep")),
            P(None, None, ("chan", "rep")),
            P(("chan", "rep")),
            P(None, ("chan", "rep")),
            P(None, ("chan", "rep")),
            P(None, "rep", "seq", "chan"),
        ),
        out_specs=P(("groups", "seq"), ("chan", "rep")),
        check_vma=False,
    )
```

```python
import functools

import jax
import jax.numpy as jnp
from jax import lax
from jax.experimental import pallas as pl
from jax.experimental.pallas import tpu as pltpu
from jax.sharding import PartitionSpec as P

GROUP = 16
LANES = 128
BLOCK = 128
PER_TILE = LANES // GROUP
WIDE = PER_TILE * BLOCK
HALO = 16
Y_SHARE = 7
GATE_PARTS = 4
MESH = pl.DeviceIdType.MESH
HIGHEST = lax.Precision.HIGHEST


def iota(shape, dim):
    return lax.broadcasted_iota(jnp.int32, shape, dim)


def masked_rows(rows):
    lane_group = iota(rows.shape, 1) // GROUP
    zero = jnp.zeros_like(rows)
    return jnp.concatenate(
        [jnp.where(lane_group == g, rows, zero) for g in range(PER_TILE)], axis=0
    )


def kernel(dims, x_hbm, sw_ref, skip_ref, rate_ref, res_ref, w_hbm, out_ref,
           xbuf, halo, ext, lhs, q_buf, base, ends, own_end, prior, rate_ch, readout, gated, wbuf,
           acc, peer, local_sem, halo_sem, end_send, end_recv, gate_send, gate_recv,
           zsend, zrecv, ysend, yrecv, rep_send, rep_recv):
    count, slabs, n_chan, n_rep, chunks, row_chunks = dims
    tok, chans = gated.shape[1], gated.shape[2]
    modes, groups = rate_ref.shape
    tiles = chans // LANES
    blocks = tok // BLOCK
    local_rows, out_cols = w_hbm.shape[2], w_hbm.shape[3]
    half = out_cols // slabs
    y_cols = out_cols // LANES * Y_SHARE // 16 * LANES
    z_cols = out_cols - y_cols
    rows = local_rows // row_chunks
    out_half = out_cols // n_rep
    slab = lax.axis_index("groups")
    seq = lax.axis_index("seq")
    chan = lax.axis_index("chan")
    rep = lax.axis_index("rep")
    other_slab = 1 - slab
    other_rep = 1 - rep

    barrier = pltpu.get_barrier_semaphore()

    def greet(target):
        pl.semaphore_signal(barrier, inc=1, device_id=target, device_id_type=MESH)

    for d in range(1, count):
        greet({"seq": lax.rem(seq + d, count)})
    for d in range(1, n_chan):
        greet({"chan": lax.rem(chan + d, n_chan)})
    greet({"groups": other_slab})
    greet({"rep": other_rep})
    pl.semaphore_wait(barrier, count + n_chan)

    def z_span(h):
        return pl.ds(pl.multiple_of(h * y_cols, LANES), z_cols)

    def y_span(h):
        return pl.ds(pl.multiple_of(h * z_cols, LANES), y_cols)

    def piece(ref, c, r, cols):
        if chunks == 1:
            return ref.at[:, :, cols]
        return ref.at[c, pl.ds(pl.multiple_of(r * rows, rows), rows), cols]

    def split(ch):
        return ch // row_chunks, ch % row_chunks

    def own_piece(ch):
        c, r = split(ch)
        return piece(w_hbm.at[:, 0], c, r, z_span(slab))

    def block_piece(b, ch, cols):
        c, r = split(ch)
        return piece(wbuf.at[b], c, r, cols)

    def target_of(direction):
        return seq + 1 if direction == 0 else seq - 1

    def can_send(direction):
        return seq < count - 1 if direction == 0 else seq > 0

    def origin(direction, k):
        return seq - 1 - k if direction == 0 else seq + 1 + k

    def has(direction, k):
        return seq - 1 - k >= 0 if direction == 0 else seq + 1 + k < count

    def z_copy(direction, k, ch, src, b):
        return pltpu.make_async_remote_copy(
            src_ref=src, dst_ref=block_piece(b, ch, z_span(slab)),
            send_sem=zsend.at[direction, k, ch], recv_sem=zrecv.at[direction, k, ch],
            device_id={"seq": target_of(direction)}, device_id_type=MESH,
        )

    def y_copy(direction, k, ch, h):
        b = origin(direction, k)
        ref = block_piece(b, ch, y_span(h))
        return pltpu.make_async_remote_copy(
            src_ref=ref, dst_ref=ref,
            send_sem=ysend.at[direction, k, ch], recv_sem=yrecv.at[direction, k, ch],
            device_id={"groups": other_slab}, device_id_type=MESH,
        )

    def halo_copy():
        return pltpu.make_async_remote_copy(
            src_ref=x_hbm.at[:, pl.ds(tok - HALO, HALO), :], dst_ref=halo,
            send_sem=halo_sem.at[0], recv_sem=halo_sem.at[1],
            device_id={"seq": seq + 1}, device_id_type=MESH,
        )

    @pl.when(seq < count - 1)
    def _():
        halo_copy().start()

    for ch in range(chunks):
        for direction in (0, 1):
            @pl.when(can_send(direction))
            def _():
                z_copy(direction, 0, ch, own_piece(ch), seq).start()

    x_copy = pltpu.make_async_copy(x_hbm, xbuf, local_sem.at[0])
    x_copy.start()
    w_copy = pltpu.make_async_copy(w_hbm.at[:, 0], wbuf.at[seq], local_sem.at[1])
    w_copy.start()
    x_copy.wait()

    @pl.when(seq > 0)
    def _():
        halo_copy().wait_recv()

    @pl.when(seq == 0)
    def _():
        halo[...] = jnp.zeros_like(halo)

    def pump(k, ch):
        for direction in (0, 1):
            @pl.when(has(direction, k))
            def _():
                b = origin(direction, k)
                landed = block_piece(b, ch, z_span(slab))
                z_copy(direction, k, ch, landed, b).wait_recv()

                @pl.when(can_send(direction))
                def _():
                    z_copy(direction, k + 1, ch, landed, b).start()

                y_copy(direction, k, ch, slab).start()

    def conv_tile(t, carry):
        cols = pl.ds(pl.multiple_of(t * LANES, LANES), LANES)

        def short(s):
            x = xbuf[s, :, cols].astype(jnp.float32)
            ext[HALO:, :] = x
            ext[:HALO, :] = halo[s, :, cols].astype(jnp.float32)
            return (
                sw_ref[s, 0:1, cols] * x
                + sw_ref[s, 1:2, cols] * ext[HALO - 1 : tok + HALO - 1, :]
                + sw_ref[s, 2:3, cols] * ext[HALO - 2 : tok + HALO - 2, :]
            )

        q_buf[:, cols] = short(0)
        product = short(1)
        product = product * short(2)

        pick_wide = (
            iota((groups, WIDE), 0) == t * PER_TILE + iota((groups, WIDE), 1) // BLOCK
        ).astype(jnp.float32)
        pick = (
            iota((groups, LANES), 0) == t * PER_TILE + iota((groups, LANES), 1) // GROUP
        ).astype(jnp.float32)

        def spread(table, which):
            return jnp.dot(table, which, precision=HIGHEST, preferred_element_type=jnp.float32)

        rate, res = rate_ref[...], res_ref[...]
        rate_rep, res_rep = spread(rate, pick_wide), spread(res, pick_wide)
        rate_c, res_c = spread(rate, pick), spread(res, pick)
        diagonal = iota((modes, LANES), 0) == iota((modes, LANES), 1) % GROUP
        rate_row = jnp.sum(jnp.where(diagonal, rate_c, 0.0), axis=0, keepdims=True)
        res_row = jnp.sum(jnp.where(diagonal, res_c, 0.0), axis=0, keepdims=True)
        ahead = (iota((BLOCK, LANES), 0) + 1).astype(jnp.float32)
        read = (res_row * jnp.exp(-rate_row * ahead)).astype(jnp.bfloat16)

        lane = iota((modes, WIDE), 1) % BLOCK
        back = ((BLOCK - lane) % BLOCK).astype(jnp.float32)
        row = jnp.sum(res_rep * jnp.exp(-rate_rep * back), axis=0, keepdims=True)
        lower = iota((BLOCK, BLOCK), 1) <= iota((BLOCK, BLOCK), 0)
        for g in range(PER_TILE):
            part = slice(g * BLOCK, (g + 1) * BLOCK)
            wide = jnp.broadcast_to(row[:, part], (BLOCK, BLOCK))
            table = pltpu.roll(wide, 0, 1, stride=1, stride_axis=0)
            lhs[:BLOCK, part] = jnp.where(lower, table, 0.0).astype(jnp.bfloat16)
        lhs[BLOCK:, :] = jnp.exp(-rate_rep * (BLOCK - 1 - lane).astype(jnp.float32)).astype(
            jnp.bfloat16
        )

        decay = jnp.exp(-rate_c * BLOCK)
        state = jnp.zeros((modes, LANES), jnp.float32)
        for b in range(blocks):
            rows_b = slice(b * BLOCK, (b + 1) * BLOCK)
            p_b = product[rows_b]
            made = jnp.dot(
                lhs[...], masked_rows(p_b.astype(jnp.bfloat16)), preferred_element_type=jnp.float32
            )
            value = made[:BLOCK] + skip_ref[:, cols] * p_b
            if b > 0:
                value = value + jnp.dot(
                    read, masked_rows(state.astype(jnp.bfloat16)), preferred_element_type=jnp.float32
                )
            base[rows_b, cols] = value
            state = decay * state + made[BLOCK:]
        own_end[:, cols] = state
        rate_ch[:, cols] = rate_c
        readout[:, cols] = read
        return carry

    steps = [(k, ch) for k in range(count - 1) for ch in range(chunks)]
    total = len(steps)
    early = 1
    part = tiles // (early + 1)
    for e in range(early + 1):
        stop = tiles if e == early else (e + 1) * part
        lax.fori_loop(e * part, stop, conv_tile, 0)
        if e < early:
            pump(*steps[e])

    def end_copy(d):
        return pltpu.make_async_remote_copy(
            src_ref=own_end, dst_ref=ends.at[seq],
            send_sem=end_send.at[d], recv_sem=end_recv.at[seq],
            device_id={"seq": seq + d}, device_id_type=MESH,
        )

    def arrived_end(source):
        return pltpu.make_async_remote_copy(
            src_ref=own_end, dst_ref=ends.at[source],
            send_sem=end_send.at[0], recv_sem=end_recv.at[source],
            device_id={"seq": seq - 1}, device_id_type=MESH,
        )

    for d in range(1, count):
        @pl.when(seq + d < count)
        def _():
            end_copy(d).start()

    pump(*steps[early])
    prior[...] = jnp.zeros_like(prior)
    for source in range(count - 1):
        @pl.when(source < seq)
        def _():
            arrived_end(source).wait_recv()
            prior[...] = prior[...] * jnp.exp(-rate_ch[...] * tok) + ends[source]

    def gate_tile(t, carry):
        cols = pl.ds(pl.multiple_of(t * LANES, LANES), LANES)
        read = readout[:, cols]
        decay = jnp.exp(-rate_ch[:, cols] * BLOCK)
        state = prior[:, cols]
        for b in range(blocks):
            rows_b = slice(b * BLOCK, (b + 1) * BLOCK)
            across = jnp.dot(
                read, masked_rows(state.astype(jnp.bfloat16)), preferred_element_type=jnp.float32
            )
            gated[chan, rows_b, cols] = (
                q_buf[rows_b, cols] * (base[rows_b, cols] + across)
            ).astype(jnp.bfloat16)
            state = decay * state
        return carry

    share = chans // GATE_PARTS

    def gate_copy(d, i):
        part_ref = gated.at[chan, :, pl.ds(i * share, share)]
        return pltpu.make_async_remote_copy(
            src_ref=part_ref, dst_ref=part_ref,
            send_sem=gate_send.at[d, i], recv_sem=gate_recv.at[chan, i],
            device_id={"chan": lax.rem(chan + d, n_chan)}, device_id_type=MESH,
        )

    def arrived_gate(d, i):
        source = lax.rem(chan + d, n_chan)
        part_ref = gated.at[source, :, pl.ds(i * share, share)]
        return pltpu.make_async_remote_copy(
            src_ref=part_ref, dst_ref=part_ref,
            send_sem=gate_send.at[0, i], recv_sem=gate_recv.at[source, i],
            device_id={"chan": source}, device_id_type=MESH,
        )

    for i in range(GATE_PARTS):
        lax.fori_loop(i * tiles // GATE_PARTS, (i + 1) * tiles // GATE_PARTS, gate_tile, 0)
        for d in range(1, n_chan):
            gate_copy(d, i).start()

    middle = max(min(2, total), total * 2 // 3)
    for e in range(early + 1, middle):
        pump(*steps[e])
    acc[...] = jnp.zeros_like(acc)
    w_copy.wait()
    for d in range(1, n_chan):
        for i in range(GATE_PARTS):
            arrived_gate(d, i).wait_recv()

    streamed = chunks > 1
    col_tile = min(512, out_cols)

    def multiply(b, ch):
        c, r = split(ch)
        a = gated[c, :, pl.ds(pl.multiple_of(b * local_rows + r * rows, LANES), rows)]

        def column(n, carry):
            cols = pl.ds(pl.multiple_of(n * col_tile, col_tile), col_tile)
            w = wbuf[b, c, pl.ds(pl.multiple_of(r * rows, rows), rows), cols]
            acc[:, cols] += jnp.dot(a, w, preferred_element_type=jnp.float32)
            return carry

        lax.fori_loop(0, out_cols // col_tile, column, 0)

    def consume(k, ch):
        for direction in (0, 1):
            @pl.when(has(direction, k))
            def _():
                y_copy(direction, k, ch, other_slab).wait_recv()
                if streamed:
                    multiply(origin(direction, k), ch)

    left_over = total - middle
    own_per = -(-chunks // left_over)
    per = -(-total // left_over)

    def both(j, carry):
        pump(j // chunks, j % chunks)
        if streamed:
            for i in range(own_per):
                ch = (j - middle) * own_per + i

                @pl.when(ch < chunks)
                def _():
                    multiply(seq, ch)

        def late(i, inner):
            old = (j - middle) * per + i

            @pl.when(old < total)
            def _():
                consume(old // chunks, old % chunks)

            return inner

        lax.fori_loop(0, per, late, 0)
        return carry

    lax.fori_loop(middle, total, both, 0)

    if not streamed:
        def whole_column(n, carry):
            cols = pl.ds(pl.multiple_of(n * half, half), half)
            for c in range(n_chan):
                w = wbuf[:, c, :, cols].reshape(count * local_rows, half)
                acc[:, cols] += jnp.dot(gated[c], w, preferred_element_type=jnp.float32)
            return carry

        lax.fori_loop(0, slabs, whole_column, 0)

    quarter = tok // 4

    def rep_copy(i, side):
        return pltpu.make_async_remote_copy(
            src_ref=acc.at[
                pl.ds(i * quarter, quarter), pl.ds(pl.multiple_of(side * out_half, LANES), out_half)
            ],
            dst_ref=peer.at[pl.ds(i * quarter, quarter), :],
            send_sem=rep_send.at[i], recv_sem=rep_recv.at[i],
            device_id={"rep": other_rep}, device_id_type=MESH,
        )

    for i in range(4):
        rep_copy(i, other_rep).start()
    mine = pl.ds(pl.multiple_of(rep * out_half, LANES), out_half)
    for i in range(4):
        rep_copy(i, other_rep).wait_recv()
        rows_i = pl.ds(i * quarter, quarter)
        out_ref[rows_i, :] = (acc[rows_i, mine] + peer[rows_i, :]).astype(jnp.bfloat16)

    for i in range(4):
        rep_copy(i, other_rep).wait_send()
    for d in range(1, n_chan):
        for i in range(GATE_PARTS):
            gate_copy(d, i).wait_send()
    for d in range(1, count):
        @pl.when(seq + d < count)
        def _():
            end_copy(d).wait_send()

    @pl.when(seq < count - 1)
    def _():
        halo_copy().wait_send()

    for ch in range(chunks):
        for direction in (0, 1):
            @pl.when(can_send(direction))
            def _():
                z_copy(direction, 0, ch, own_piece(ch), seq).wait_send()

    def drain(j, carry):
        k, ch = j // chunks, j % chunks
        for direction in (0, 1):
            @pl.when(has(direction, k))
            def _():
                y_copy(direction, k, ch, slab).wait_send()

                @pl.when(can_send(direction))
                def _():
                    b = origin(direction, k)
                    z_copy(direction, k + 1, ch, block_piece(b, ch, z_span(slab)), b).wait_send()
        return carry

    lax.fori_loop(0, total, drain, 0)


def per_device(projected, short_weight, skip_gain, pole_rate, residue, out_weight):
    tok, _, chans = projected.shape
    modes, groups = pole_rate.shape
    n_chan, _, local_rows, out_cols = out_weight.shape
    count, slabs = lax.axis_size("seq"), lax.axis_size("groups")
    n_rep = lax.axis_size("rep")
    row_chunks = max(1, local_rows // 256)
    chunks = n_chan * row_chunks if local_rows % LANES == 0 else 1
    dims = (count, slabs, n_chan, n_rep, chunks, row_chunks)
    f32, bf16 = jnp.float32, jnp.bfloat16
    dma = pltpu.SemaphoreType.DMA
    anywhere = pl.BlockSpec(memory_space=pl.ANY)
    vmem = pl.BlockSpec(memory_space=pltpu.VMEM)
    return pl.pallas_call(
        functools.partial(kernel, dims),
        in_specs=[anywhere, vmem, vmem, vmem, vmem, anywhere],
        out_specs=vmem,
        out_shape=jax.ShapeDtypeStruct((tok, out_cols // n_rep), bf16),
        scratch_shapes=[
            pltpu.VMEM((3, tok, chans), bf16),
            pltpu.VMEM((3, HALO, chans), bf16),
            pltpu.VMEM((tok + HALO, LANES), f32),
            pltpu.VMEM((BLOCK + modes, WIDE), bf16),
            pltpu.VMEM((tok, chans), f32),
            pltpu.VMEM((tok, chans), f32),
            pltpu.VMEM((count, modes, chans), f32),
            pltpu.VMEM((modes, chans), f32),
            pltpu.VMEM((modes, chans), f32),
            pltpu.VMEM((modes, chans), f32),
            pltpu.VMEM((BLOCK, chans), bf16),
            pltpu.VMEM((n_chan, tok, chans), bf16),
            pltpu.VMEM((count, n_chan, local_rows, out_cols), bf16),
            pltpu.VMEM((tok, out_cols), f32),
            pltpu.VMEM((tok, out_cols // n_rep), f32),
            dma((2,)),
            dma((2,)),
            dma((count,)),
            dma((count,)),
            dma((n_chan, GATE_PARTS)),
            dma((n_chan, GATE_PARTS)),
            dma((2, count, chunks)),
            dma((2, count, chunks)),
            dma((2, count, chunks)),
            dma((2, count, chunks)),
            dma((4,)),
            dma((4,)),
        ],
        compiler_params=pltpu.CompilerParams(
            collective_id=0, has_side_effects=True, vmem_limit_bytes=60 * 1024 * 1024
        ),
        name="hyena",
    )(
        projected.transpose(1, 0, 2), short_weight, skip_gain[None], pole_rate, residue, out_weight
    )


def solution(mesh):
    return jax.shard_map(
        per_device,
        mesh=mesh,
        in_specs=(
            P(("groups", "seq"), None, ("chan", "rep")),
            P(None, None, ("chan", "rep")),
            P(("chan", "rep")),
            P(None, ("chan", "rep")),
            P(None, ("chan", "rep")),
            P(None, "rep", "seq", "chan"),
        ),
        out_specs=P(("groups", "seq"), ("chan", "rep")),
        check_vma=False,
    )
```
